512 devices in a mesh: ens: 32 (over x_hi, z, core), tile: 16 (over x_lo, y).
Axes of the slice: x: 4 (x_hi: 2, x_lo: 2; x = x_hi * 2 + x_lo), y: 8, z: 8, core: 2. Of those that a mesh axis runs over, the one named last changes fastest.
Arguments:
- coords: float32 [256, 3, 3200], P('ens', None, 'tile'), may hold values from -6 to 6
- counts: int32 [3200, 3200], P('tile'), may hold values from 0 to 63, as said below
- segments: int32 [3200], replicated, may hold values from 0 to 7, never falling along the last dimension, each value on 1 to 800 neighbouring positions
Outputs:
- gradient: float32 [256, 3, 3200], P('ens', None, 'tile')
The draws below stay inside these ranges and needn't reach their ends.
Inputs may be any that keep to these rules, and one draw needn't show every extreme that they name: counts is symmetric: counts[i, j] == counts[j, i].
All inputs are finite; a program needn't handle non-finite values.
Results may differ from the reference program's by a relative error of at most 0.00011.
Values sent between devices are 32-bit elements; how exact they have to be, the bound alone decides.
A program may use at most 64 MiB of HBM per device.

```python
import math
import jax
import jax.numpy as jnp
import numpy as np
from jax import lax

BEADS = 3200
SEGS = 8
STRUCTS = 256


def draw_counts(key, part):
    raw = jax.random.randint(key, (BEADS, BEADS), 0, 64, dtype=jnp.int32)
    rows = lax.broadcasted_iota(jnp.int32, (BEADS, BEADS), 0)
    cols = lax.broadcasted_iota(jnp.int32, (BEADS, BEADS), 1)
    raw = jnp.where((rows == 0) & (cols == 1), 63, raw)
    raw = jnp.where((rows == 0) & (cols == 2), 0, raw)
    return jnp.where(rows <= cols, raw, raw.T)


def shard_levels(stream_key, dims, shards, low, high):
    gain, own = 1.0, jax.random.fold_in(stream_key, 6)
    for dim, blocks in shards:
        steps = jnp.exp(jax.random.uniform(jax.random.fold_in(own, dim), (blocks,), jnp.float32, low / len(shards), high / len(shards)))
        gain = gain * jnp.repeat(steps, dims[dim] // blocks).reshape([-1 if axis == dim else 1 for axis in range(len(dims))])
    return gain


def profile(number_of, total, reach, lean):
    weights = [(1 << 20) // math.isqrt(grade ** lean) + 1 for grade in range(2, number_of + 1)]
    surplus, given = total - reach - (number_of - 1), [1] * (number_of - 1)
    while surplus > 0:
        free = [i for i in range(number_of - 1) if given[i] < reach]
        pool, remaining = sum([weights[i] for i in free]), surplus
        for i in free:
            more = min(reach - given[i], max(1, remaining * weights[i] // pool), surplus)
            given[i] = given[i] + more
            surplus = surplus - more
    return np.array([reach] + given)


def ragged(own_key, count, total, bound, lean):
    if count == 2:
        one = jax.random.randint(own_key, (), max(1, total - bound), min(bound, total - 1) + 1)
        return jnp.stack([one, total - one])
    lengths = jnp.asarray(profile(count, total, bound, lean), jnp.int32)
    pairs = (count - 1) // 2
    source_of, taker = lengths[1:1 + 2 * pairs:2], lengths[2:2 + 2 * pairs:2]
    slack = jnp.minimum(source_of - 1, bound - taker)
    passed = jax.random.randint(jax.random.fold_in(own_key, 1), (pairs,), 0, 1 << 20) % (slack + 1)
    lengths = lengths.at[1:1 + 2 * pairs:2].set(source_of - passed).at[2:2 + 2 * pairs:2].set(taker + passed)
    return lengths[jax.random.permutation(jax.random.fold_in(own_key, 2), count)]


def scatter_about(stream_key, dims, width, limit, shards=(), kind=jnp.bfloat16):
    array = width * jax.random.normal(stream_key, dims, jnp.float32)
    if shards:
        array = array * shard_levels(stream_key, dims, shards, -0.22, 0.18)
    return jnp.clip(array, -limit, limit).astype(kind)


def setup_inputs(seed: int = 0) -> dict:
    splits = jax.random.split(jax.random.key(seed), 4)
    return {
        "coords": scatter_about(splits[0], (STRUCTS, 3, BEADS), 1.0, 6.0, ((0, 32), (2, 16)), jnp.float32),
        "counts": draw_counts(jax.random.fold_in(splits[3], 71), 0),
        "segments": jnp.searchsorted(jnp.cumsum(ragged(splits[2], SEGS, BEADS, BEADS // 4, 1)), jnp.arange(BEADS), side="right").astype(jnp.int32),
    }


def pair_sigmoid(rows_xyz, all_xyz):
    gap = rows_xyz[:, :, None] - all_xyz[:, None, :]
    dist = jnp.sum(gap * gap, axis=0)
    return jax.nn.sigmoid(1.0 * (6.0 - dist))


def reference(coords, counts, segments):
    beads = coords.shape[2]
    index = jnp.arange(beads, dtype=jnp.int32)
    same = segments[:, None] == segments[None, :]
    weight = jnp.where(index[:, None] == index[None, :], 0.0, jnp.where(same, 1.0, 0.3)).astype(jnp.float32)
    count_f = counts.astype(jnp.float32)
    target = count_f / (count_f + 8.0)

    def accumulate(total, xyz):
        return total + pair_sigmoid(xyz, xyz), None

    total, unused = lax.scan(accumulate, jnp.zeros((beads, beads), jnp.float32), coords)
    pbar = total / coords.shape[0]
    weighted = weight * (pbar - target)

    def grad_one(xyz):
        sig = pair_sigmoid(xyz, xyz)
        term = weighted * sig * (1.0 - sig)
        rowsum = jnp.sum(term, axis=1)
        mixed = jnp.dot(xyz, term.T, precision=lax.Precision.HIGHEST, preferred_element_type=jnp.float32)
        return -(1.0 / 16) * (rowsum[None, :] * xyz - mixed)

    return lax.map(grad_one, coords)
```

```python
import functools

import jax
import jax.numpy as jnp
from jax import lax
from jax.experimental import pallas as pl
from jax.experimental.pallas import tpu as pltpu
from jax.sharding import PartitionSpec as P

MESH = pl.DeviceIdType.MESH
LANES = 128
WINDOW = 384
F32 = jnp.float32


def up(n, m):
    return (n + m - 1) // m * m


def partner_order(n):
    half = n // 2
    pairs = [(a, b) for a in range(2) for b in range(half) if (a, b) != (0, 0)]
    return sorted(pairs, key=lambda p: p[0] + min(p[1], half - p[1]))


def member(index, offset, n):
    a, b = offset
    half = n // 2
    return lax.rem(lax.div(index, half) + a, 2) * half + lax.rem(lax.rem(index, half) + b, half)


def against(a, b):
    return lax.dot_general(a, b, (((1,), (1,)), ((), ())), preferred_element_type=F32)


def kernel(
    n, structs, coords_ref, counts_ref, seg_ref, out_ref,
    mine, tiles, rows_in, cols_in, row_t, col_t, row_c, col_c, tanhs,
    window, rest, scale, weights, part, other, grad_t, grad_s, parts_in,
    tile_send, tile_recv, row_send, row_recv, col_send, col_recv, core_send, core_recv,
    out_send, out_recv, count_sem,
):
    _, local_n, rows = coords_ref.shape
    beads = counts_ref.shape[1]
    width = mine.shape[1]
    lanes = n * local_n
    second = rows - LANES
    halves = ((0, LANES), (LANES, second))
    cuts = (0, 3 * LANES, grad_s.shape[2])
    order = partner_order(n)
    ens = lax.axis_index("ens")
    t = lax.axis_index("tile")
    me, core = lax.div(ens, 2), lax.rem(ens, 2)

    def window_of(tile):
        first = tile * rows
        start = jnp.minimum(lax.div(first, LANES) * LANES, beads - WINDOW)
        return pl.multiple_of(start, LANES), first - start

    col_start, col_off = window_of(me)
    row_start, row_off = window_of(t)
    counts_copy = pltpu.make_async_copy(counts_ref.at[:, pl.ds(col_start, WINDOW)], window, count_sem)
    counts_copy.start()

    barrier = pltpu.get_barrier_semaphore()
    for offset in order:
        pl.semaphore_signal(barrier, inc=1, device_id={"tile": member(t, offset, n)}, device_id_type=MESH)
        pl.semaphore_signal(
            barrier, inc=1, device_id={"ens": member(me, offset, n) * 2 + core}, device_id_type=MESH
        )
    pl.semaphore_signal(barrier, inc=1, device_id={"ens": me * 2 + 1 - core}, device_id_type=MESH)

    for c in range(3):
        mine[:, c * rows : (c + 1) * rows] = coords_ref[c]
    mine[:, 3 * rows :] = jnp.zeros((local_n, width - 3 * rows), F32)
    part[...] = jnp.zeros_like(part)
    rows_in[me] = mine[...]

    pl.semaphore_wait(barrier, 2 * len(order) + 1)

    def to_tile(offset):
        p = member(t, offset, n)
        return pltpu.make_async_remote_copy(
            mine, tiles.at[t], tile_send.at[p], tile_recv.at[t], device_id={"tile": p}, device_id_type=MESH
        )

    def from_tile(p):
        return pltpu.make_async_remote_copy(
            mine, tiles.at[p], tile_send.at[p], tile_recv.at[p], device_id={"tile": p}, device_id_type=MESH
        )

    def to_row(offset):
        p = member(me, offset, n)
        return pltpu.make_async_remote_copy(
            mine, rows_in.at[me], row_send.at[p], row_recv.at[me],
            device_id={"ens": p * 2 + core}, device_id_type=MESH,
        )

    def from_row(p):
        return pltpu.make_async_remote_copy(
            mine, rows_in.at[p], row_send.at[p], row_recv.at[p],
            device_id={"ens": p * 2 + core}, device_id_type=MESH,
        )

    def to_col(source, p):
        return pltpu.make_async_remote_copy(
            source, cols_in.at[me], col_send.at[p], col_recv.at[me],
            device_id={"ens": p * 2 + core}, device_id_type=MESH,
        )

    def from_col(p):
        return pltpu.make_async_remote_copy(
            mine, cols_in.at[p], col_send.at[p], col_recv.at[p],
            device_id={"ens": p * 2 + core}, device_id_type=MESH,
        )

    for offset in order:
        to_tile(offset).start()

    @pl.when(t != me)
    def _():
        to_col(mine, t).start()

    for offset in order:
        to_row(offset).start()

    counts_copy.wait()
    lane_ids = lax.broadcasted_iota(jnp.int32, (rows, WINDOW), 1)
    bead_ids = lax.broadcasted_iota(jnp.int32, (rows, WINDOW), 0)
    pick_col = lane_ids == bead_ids + col_off
    pick_row = (lane_ids == bead_ids + row_off).astype(F32).astype(jnp.bfloat16)
    seg_col = jnp.sum(
        jnp.where(pick_col, seg_ref[:, pl.ds(col_start, WINDOW)].astype(F32), 0.0), axis=1, keepdims=True
    )
    seg_rows = jnp.broadcast_to(
        seg_ref[:, pl.ds(row_start, WINDOW)].astype(F32), (8, WINDOW)
    ).astype(jnp.bfloat16)
    pick_col = pick_col.astype(F32).astype(jnp.bfloat16)
    for h, (first, size) in enumerate(halves):
        counts_f = window[first : first + size, :].astype(F32).astype(jnp.bfloat16)
        count = against(pick_col, counts_f)
        seg_row = against(seg_rows, pick_row[first : first + size, :])[0:1, :]
        same = seg_col == seg_row
        diagonal = (
            me * rows + lax.broadcasted_iota(jnp.int32, (rows, size), 0)
            == t * rows + first + lax.broadcasted_iota(jnp.int32, (rows, size), 1)
        )
        weight = jnp.where(diagonal, 0.0, jnp.where(same, 1.0, 0.3))
        rest[h, :, 0:size] = 0.5 - count / (count + 8.0)
        scale[h, :, 0:size] = weight * (-1.0 / 64.0)
        if size < LANES:
            rest[h, :, size:] = jnp.zeros((rows, LANES - size), F32)
            scale[h, :, size:] = jnp.zeros((rows, LANES - size), F32)

    for offset in order:
        p = member(t, offset, n)
        from_tile(p).wait_recv()

        @pl.when(p != me)
        def _():
            to_col(tiles.at[p], p).start()

        @pl.when(p == me)
        def _():
            cols_in[me] = tiles[me]

    @pl.when(t == me)
    def _():
        cols_in[me] = mine[...]

    def turn(source, target):
        for b in range(width // LANES):
            block = source[:, :, b * LANES : (b + 1) * LANES].reshape(lanes, LANES)
            target[b * LANES : (b + 1) * LANES, :] = block.T

    def norms(target, bias):
        x, y, z = (target[c * rows : (c + 1) * rows, :] for c in range(3))
        return bias - 0.5 * (x * x + y * y + z * z)

    for offset in order:
        from_row(member(me, offset, n)).wait_recv()
    turn(rows_in, row_t)
    row_c[...] = norms(row_t, 3.0)

    for offset in order:
        from_col(member(me, offset, n)).wait_recv()
    turn(cols_in, col_t)
    col_c[...] = norms(col_t, 0.0)

    blocks = rows // 8
    lane = lax.broadcasted_iota(jnp.int32, (8, LANES), 1)

    def col_block(j):
        return [col_t[pl.ds(pl.multiple_of(c * rows + 8 * j, 8), 8), :] for c in range(3)]

    def row_of(ref, r):
        return jnp.broadcast_to(ref[pl.ds(r, 1), :], (8, lanes))

    def sigmoids(h):
        first, size = halves[h]

        def row_block(b, carry):
            i = first + 8 * b
            at = [[row_of(row_t, c * rows + i + q) for c in range(3)] for q in range(8)]
            bias = [row_of(row_c, i + q) for q in range(8)]

            def pairs(j, carry):
                x, y, z = col_block(j)
                own = pl.ds(pl.multiple_of(8 * j, 8), 8)
                cj = col_c[own, :]
                total = part[h, own, :]
                for q in range(8):
                    xi, yi, zi = at[q]
                    v = jnp.tanh(((bias[q] + cj) + xi * x) + (yi * y + zi * z))
                    tanhs[first // 8 + b, j, q] = v
                    total = jnp.where(lane == 8 * b + q, jnp.sum(v, axis=1, keepdims=True), total)
                part[h, own, :] = total
                return carry

            return lax.fori_loop(0, blocks, pairs, carry, unroll=25)

        lax.fori_loop(0, size // 8, row_block, 0)

    def swap(h):
        return pltpu.make_async_remote_copy(
            part.at[h], other.at[h], core_send.at[h], core_recv.at[h],
            device_id={"ens": me * 2 + 1 - core}, device_id_type=MESH,
        )

    def gradients(h):
        first, size = halves[h]
        pitch = LANES if h == 0 else second

        def row_block(b, carry):
            i = first + 8 * b
            down = [[], [], []]
            for group in range(0, 8, 2):
                members = range(group, group + 2)

                def pairs(j, sums):
                    x, y, z = col_block(j)
                    w = weights[h, pl.ds(pl.multiple_of(8 * j, 8), 8), :]
                    w = pltpu.roll(w, lax.rem(LANES - 8 * b, LANES), 1)
                    new = []
                    for q, (s, sx, sy, sz) in zip(members, sums):
                        v = tanhs[first // 8 + b, j, q]
                        wq = jnp.broadcast_to(w[:, q : q + 1], (8, lanes))
                        g = wq - wq * (v * v)
                        new.append((s + g, sx + g * x, sy + g * y, sz + g * z))
                    return tuple(new)

                zero = jnp.zeros((8, lanes), F32)
                sums = lax.fori_loop(0, blocks, pairs, ((zero,) * 4,) * 2, unroll=25)
                for c in range(3):
                    for q, total in zip(members, sums):
                        down[c].append(
                            jnp.sum(row_of(row_t, c * rows + i + q) * total[0] - total[c + 1], axis=0, keepdims=True)
                        )
            for c in range(3):
                at = pl.multiple_of(cuts[h] + c * pitch + 8 * b, 8)
                grad_t[pl.ds(at, 8), :] = jnp.concatenate(down[c], axis=0)
            return carry

        lax.fori_loop(0, size // 8, row_block, 0)

    def to_owner(h, p):
        cut = slice(cuts[h], cuts[h + 1])
        return pltpu.make_async_remote_copy(
            grad_s.at[p, :, cut], parts_in.at[me, :, cut], out_send.at[h, p], out_recv.at[h, me],
            device_id={"ens": p * 2 + core}, device_id_type=MESH,
        )

    def from_sharer(h, p):
        cut = slice(cuts[h], cuts[h + 1])
        return pltpu.make_async_remote_copy(
            grad_s.at[p, :, cut], parts_in.at[p, :, cut], out_send.at[h, p], out_recv.at[h, p],
            device_id={"ens": p * 2 + core}, device_id_type=MESH,
        )

    for h in range(2):
        sigmoids(h)
        swap(h).start()
    used = cuts[1] + 3 * second
    grad_t[used:, :] = jnp.zeros((grad_t.shape[0] - used, lanes), F32)
    for h in range(2):
        swap(h).wait()
        mean = (part[h] + other[h]) * (1.0 / structs) * 0.5
        weights[h] = scale[h] * (rest[h] + mean)
        gradients(h)
        for b in range(cuts[h] // LANES, cuts[h + 1] // LANES):
            block = grad_t[b * LANES : (b + 1) * LANES, :].T
            grad_s[:, :, b * LANES : (b + 1) * LANES] = block.reshape(n, local_n, LANES)
        for offset in reversed(order):
            to_owner(h, member(me, offset, n)).start()

    for h, (first, size) in enumerate(halves):
        pitch = LANES if h == 0 else second
        total = grad_s[me, :, cuts[h] : cuts[h + 1]]
        for offset in order:
            p = member(me, offset, n)
            from_sharer(h, p).wait_recv()
            total = total + parts_in[p, :, cuts[h] : cuts[h + 1]]
        for c in range(3):
            out_ref[c, :, first : first + size] = total[:, c * pitch : c * pitch + size]

    for offset in order:
        to_tile(offset).wait_send()
        to_row(offset).wait_send()
        p = member(me, offset, n)
        for h in range(2):
            to_owner(h, p).wait_send()
        to_col(mine, p).wait_send()


def solution(mesh):
    n = mesh.shape["tile"]

    def on_device(coords, counts, segments):
        local_n, _, rows = coords.shape
        structs = local_n * mesh.shape["ens"]
        lanes = n * local_n
        width = up(3 * rows, LANES)
        wide = 3 * LANES + up(3 * (rows - LANES), LANES)
        blocks = rows // 8
        vmem, dma = pltpu.VMEM, pltpu.SemaphoreType.DMA
        out = pl.pallas_call(
            functools.partial(kernel, n, structs),
            out_shape=jax.ShapeDtypeStruct((3, local_n, rows), F32),
            in_specs=[
                pl.BlockSpec(memory_space=pltpu.VMEM),
                pl.BlockSpec(memory_space=pl.ANY),
                pl.BlockSpec(memory_space=pltpu.VMEM),
            ],
            out_specs=pl.BlockSpec(memory_space=pltpu.VMEM),
            scratch_shapes=[
                vmem((local_n, width), F32),
                vmem((n, local_n, width), F32),
                vmem((n, local_n, width), F32),
                vmem((n, local_n, width), F32),
                vmem((width, lanes), F32),
                vmem((width, lanes), F32),
                vmem((rows, lanes), F32),
                vmem((rows, lanes), F32),
                vmem((blocks, blocks, 8, 8, lanes), F32),
                vmem((rows, WINDOW), jnp.int32),
                vmem((2, rows, LANES), F32),
                vmem((2, rows, LANES), F32),
                vmem((2, rows, LANES), F32),
                vmem((2, rows, LANES), F32),
                vmem((2, rows, LANES), F32),
                vmem((wide, lanes), F32),
                vmem((n, local_n, wide), F32),
                vmem((n, local_n, wide), F32),
                dma((n,)), dma((n,)), dma((n,)), dma((n,)), dma((n,)), dma((n,)),
                dma((2,)), dma((2,)), dma((2, n)), dma((2, n)), dma,
            ],
            compiler_params=pltpu.CompilerParams(
                collective_id=0, has_side_effects=True, vmem_limit_bytes=60 * 1024 * 1024
            ),
        )(coords.transpose(1, 0, 2), counts, segments.reshape(1, -1))
        return out.transpose(1, 0, 2)

    return jax.shard_map(
        on_device,
        mesh=mesh,
        in_specs=(P("ens", None, "tile"), P("tile", None), P()),
        out_specs=P("ens", None, "tile"),
        check_vma=False,
    )
```

```python
import functools

import jax
import jax.numpy as jnp
from jax import lax
from jax.experimental import pallas as pl
from jax.experimental.pallas import tpu as pltpu
from jax.sharding import PartitionSpec as P

MESH = pl.DeviceIdType.MESH
LANES = 128
WINDOW = 384
GROUP = 5
CHUNK = 8 * GROUP
F32 = jnp.float32


def up(n, m):
    return (n + m - 1) // m * m


def partner_order(n):
    half = n // 2
    pairs = [(a, b) for a in range(2) for b in range(half) if (a, b) != (0, 0)]
    return sorted(pairs, key=lambda p: p[0] + min(p[1], half - p[1]))


def member(index, offset, n):
    a, b = offset
    half = n // 2
    return lax.rem(lax.div(index, half) + a, 2) * half + lax.rem(lax.rem(index, half) + b, half)


def against(a, b):
    return lax.dot_general(a, b, (((1,), (1,)), ((), ())), preferred_element_type=F32)


def kernel(
    n, structs, coords_ref, counts_ref, seg_ref, out_ref,
    mine, tiles, rows_in, cols_in, row_t, col_t, row_c, col_c, tanhs,
    window, rest, scale, weights, part, other, grad_t, grad_s, parts_in,
    tile_send, tile_pass, tile_recv, row_send, row_pass, row_recv, col_send, col_recv, core_send, core_recv,
    out_send, out_recv, count_sem,
):
    _, local_n, rows = coords_ref.shape
    beads = counts_ref.shape[1]
    lanes = n * local_n
    blocks = rows // 8
    chunks = rows // CHUNK
    order = partner_order(n)
    line = [offset for offset in order if offset[0] == 0]
    over = [offset for offset in order if offset[0] == 1]
    near = line + over[:1]
    split = max(1, 2 * chunks // 5)
    parts = ((0, split), (split, chunks))
    ens = lax.axis_index("ens")
    t = lax.axis_index("tile")
    me, core = lax.div(ens, 2), lax.rem(ens, 2)

    def window_of(tile):
        first = tile * rows
        start = jnp.minimum(lax.div(first, LANES) * LANES, beads - WINDOW)
        return pl.multiple_of(start, LANES), first - start

    col_start, col_off = window_of(me)
    row_start, row_off = window_of(t)
    counts_copy = pltpu.make_async_copy(counts_ref.at[:, pl.ds(col_start, WINDOW)], window, count_sem)
    counts_copy.start()

    barrier = pltpu.get_barrier_semaphore()
    for offset in near:
        pl.semaphore_signal(barrier, inc=1, device_id={"tile": member(t, offset, n)}, device_id_type=MESH)
    for offset in order:
        pl.semaphore_signal(
            barrier, inc=1, device_id={"ens": member(me, offset, n) * 2 + core}, device_id_type=MESH
        )
    pl.semaphore_signal(barrier, inc=1, device_id={"ens": me * 2 + 1 - core}, device_id_type=MESH)

    for h in range(chunks):
        for c in range(3):
            mine[h, :, c * CHUNK : (c + 1) * CHUNK] = coords_ref[c, :, h * CHUNK : (h + 1) * CHUNK]
        mine[h, :, 3 * CHUNK :] = jnp.zeros((local_n, LANES - 3 * CHUNK), F32)
    rows_in[me] = mine[...]

    pl.semaphore_wait(barrier, len(near) + len(order) + 1)

    def of(part):
        return slice(parts[part][0], parts[part][1])

    def tile_copy(a, source, sem, p, slot):
        return pltpu.make_async_remote_copy(
            source.at[of(a)], tiles.at[slot, of(a)], sem, tile_recv.at[a, slot],
            device_id={"tile": p}, device_id_type=MESH,
        )

    def row_copy(source, sem, p, slot):
        return pltpu.make_async_remote_copy(
            source, rows_in.at[slot], sem, row_recv.at[slot],
            device_id={"ens": p * 2 + core}, device_id_type=MESH,
        )

    def col_copy(a, source, p, slot):
        return pltpu.make_async_remote_copy(
            source.at[of(a)], cols_in.at[slot, of(a)], col_send.at[a, p], col_recv.at[a, slot],
            device_id={"ens": p * 2 + core}, device_id_type=MESH,
        )

    tile_over = member(t, over[0], n)
    row_over = member(me, over[0], n)

    def send_tiles(a):
        for offset in near:
            p = member(t, offset, n)
            tile_copy(a, mine, tile_send.at[a, p], p, t).start()

        @pl.when(t != me)
        def _():
            col_copy(a, mine, t, me).start()

        @pl.when(t == me)
        def _():
            cols_in[me, of(a)] = mine[of(a)]

    def relay_tiles(a, offsets, on):
        for offset in offsets:
            p = member(t, offset, n)
            tile_copy(a, mine, tile_send.at[a, p], p, p).wait_recv()
            if on:
                tile_copy(a, tiles.at[p], tile_pass.at[a, p], tile_over, p).start()

            @pl.when(p != me)
            def _():
                col_copy(a, tiles.at[p], p, me).start()

            @pl.when(p == me)
            def _():
                cols_in[me, of(a)] = tiles[me, of(a)]

    send_tiles(0)
    for offset in near:
        p = member(me, offset, n)
        row_copy(mine, row_send.at[p], p, me).start()
    send_tiles(1)
    part[...] = jnp.zeros_like(part)

    counts_copy.wait()
    lane_ids = lax.broadcasted_iota(jnp.int32, (rows, WINDOW), 1)
    bead_ids = lax.broadcasted_iota(jnp.int32, (rows, WINDOW), 0)
    pick_row = lane_ids == bead_ids + row_off
    seg_row = jnp.sum(
        jnp.where(pick_row, seg_ref[:, pl.ds(row_start, WINDOW)].astype(F32), 0.0), axis=1, keepdims=True
    )
    seg_cols = jnp.broadcast_to(
        seg_ref[:, pl.ds(col_start, WINDOW)].astype(F32), (8, WINDOW)
    ).astype(jnp.bfloat16)
    counts_f = window[...].astype(F32).astype(jnp.bfloat16)
    pick_ids = lax.broadcasted_iota(jnp.int32, (LANES, WINDOW), 1)
    pick_bead = lax.broadcasted_iota(jnp.int32, (LANES, WINDOW), 0)
    for h in range(chunks):
        pick = (pick_ids == pick_bead + col_off + h * CHUNK) & (pick_bead < CHUNK)
        pick = pick.astype(F32).astype(jnp.bfloat16)
        count = against(counts_f, pick)
        same = seg_row == against(seg_cols, pick)[0:1, :]
        bead = lax.broadcasted_iota(jnp.int32, (rows, LANES), 1)
        diagonal = t * rows + lax.broadcasted_iota(jnp.int32, (rows, LANES), 0) == me * rows + h * CHUNK + bead
        weight = jnp.where(diagonal, 0.0, jnp.where(same, 1.0, 0.3))
        rest[h] = 0.5 - count / (count + 8.0)
        scale[h] = weight * (-1.0 / 64.0)

    relay_tiles(0, line, True)
    for offset in line:
        p = member(me, offset, n)
        row_copy(mine, row_send.at[p], p, p).wait_recv()
        row_copy(rows_in.at[p], row_pass.at[p], row_over, p).start()
    relay_tiles(0, over, False)
    relay_tiles(1, line, True)
    relay_tiles(1, over, False)

    def turn(block, target, h):
        block = block.reshape(lanes, LANES).T
        for c in range(3):
            at = pl.multiple_of(c * rows + h * CHUNK, 8)
            target[pl.ds(at, CHUNK), :] = block[c * CHUNK : (c + 1) * CHUNK, :]

    def norms(source, target, bias, h):
        x, y, z = (source[pl.ds(pl.multiple_of(c * rows + h * CHUNK, 8), CHUNK), :] for c in range(3))
        target[pl.ds(pl.multiple_of(h * CHUNK, 8), CHUNK), :] = bias - 0.5 * (x * x + y * y + z * z)

    lane = lax.broadcasted_iota(jnp.int32, (8, LANES), 1)

    def spread(ref, r):
        return jnp.broadcast_to(ref[pl.ds(r, 1), :], (8, lanes))

    def sigmoids(h):
        def col_block(b, carry):
            j = h * CHUNK + 8 * b
            at = [[spread(col_t, c * rows + j + q) for c in range(3)] for q in range(8)]
            bias = [spread(col_c, j + q) for q in range(8)]
            for k in range(blocks):
                own = slice(8 * k, 8 * k + 8)
                x, y, z = (row_t[c * rows + 8 * k : c * rows + 8 * k + 8, :] for c in range(3))
                ci = row_c[own, :]
                for q in range(8):
                    xj, yj, zj = at[q]
                    v = jnp.tanh(((bias[q] + ci) + xj * x) + (yj * y + zj * z))
                    tanhs[h * GROUP + b, k, q] = v
                    part[h, own, 8 * b + q : 8 * b + q + 1] = jnp.sum(v, axis=1, keepdims=True)
            return carry

        for b in range(GROUP):
            col_block(b, 0)

    def swap(h):
        return pltpu.make_async_remote_copy(
            part.at[h], other.at[h], core_send.at[h], core_recv.at[h],
            device_id={"ens": me * 2 + 1 - core}, device_id_type=MESH,
        )

    def weigh(h):
        mean = (part[h] + other[h]) * (0.5 / structs)
        weights[h] = scale[h] * (rest[h] + mean)

    def out_copy(g, p, slot):
        return pltpu.make_async_remote_copy(
            grad_s.at[g, p], parts_in.at[g, slot], out_send.at[g, p], out_recv.at[g, slot],
            device_id={"ens": p * 2 + core}, device_id_type=MESH,
        )

    def gather_pairs(g, acc, h):
        at = [pl.multiple_of(CHUNK * g + 8 * k, 8) for k in range(GROUP)]
        for b in range(GROUP):
            w = [weights[h, pl.ds(at[k], 8), :] for k in range(GROUP)]
            for q in range(8):
                j = h * CHUNK + 8 * b + q
                x, y, z = (spread(col_t, c * rows + j) for c in range(3))
                for k in range(GROUP):
                    v = tanhs[h * GROUP + b, GROUP * g + k, q]
                    wq = jnp.broadcast_to(w[k][:, 8 * b + q : 8 * b + q + 1], (8, lanes))
                    d = wq - wq * (v * v)
                    s, sx, sy, sz = acc[k]
                    acc[k] = [s + d, sx + d * x, sy + d * y, sz + d * z]
        return acc

    def row_group(g, wait=False):
        acc = [[jnp.zeros((8, lanes), F32)] * 4 for k in range(GROUP)]
        for h in range(chunks - 1):
            acc = gather_pairs(g, acc, h)

        if wait:
            swap(chunks - 1).wait()
            weigh(chunks - 1)

        acc = gather_pairs(g, acc, chunks - 1)
        for k in range(GROUP):
            for c in range(3):
                xi = row_t[pl.ds(pl.multiple_of(c * rows + CHUNK * g + 8 * k, 8), 8), :]
                grad_t[c * CHUNK + 8 * k : c * CHUNK + 8 * k + 8, :] = xi * acc[k][0] - acc[k][c + 1]
        grad_s[g] = grad_t[...].T.reshape(n, local_n, LANES)
        for offset in reversed(order):
            out_copy(g, member(me, offset, n), me).start()

    for offset in over:
        p = member(me, offset, n)
        row_copy(mine, row_send.at[p], p, p).wait_recv()
    for h in range(chunks):
        turn(rows_in[:, h], row_t, h)
        norms(row_t, row_c, 3.0, h)

    def first_pass(h, carry):
        turn(cols_in[:, h], col_t, h)
        norms(col_t, col_c, 0.0, h)
        sigmoids(h)
        swap(h).start()
        return carry

    for a, span in enumerate(parts):
        for offset in order:
            p = member(me, offset, n)
            col_copy(a, mine, p, p).wait_recv()
        lax.fori_loop(span[0], span[1], first_pass, 0)
    grad_t[3 * CHUNK :, :] = jnp.zeros((LANES - 3 * CHUNK, lanes), F32)
    for h in range(chunks - 1):
        swap(h).wait()
        weigh(h)
    row_group(0, True)

    @pl.loop(1, chunks)
    def _(g):
        row_group(g)


    def collect(g, carry):
        total = grad_s[g, me]
        for offset in order:
            p = member(me, offset, n)
            out_copy(g, p, p).wait_recv()
            total = total + parts_in[g, p]
        grad_s[g, me] = total
        return carry

    lax.fori_loop(0, chunks, collect, 0)
    for g in range(chunks):
        for c in range(3):
            out_ref[c, :, g * CHUNK : (g + 1) * CHUNK] = grad_s[g, me, :, c * CHUNK : (c + 1) * CHUNK]

    def drain(g, carry):
        for offset in order:
            p = member(me, offset, n)
            out_copy(g, p, p).wait_send()
        return carry

    lax.fori_loop(0, chunks, drain, 0)
    for offset in near:
        p, q = member(me, offset, n), member(t, offset, n)
        row_copy(mine, row_send.at[p], p, me).wait_send()
        for a in range(2):
            tile_copy(a, mine, tile_send.at[a, q], q, t).wait_send()
    for offset in line:
        p, q = member(me, offset, n), member(t, offset, n)
        row_copy(rows_in.at[p], row_pass.at[p], row_over, p).wait_send()
        for a in range(2):
            tile_copy(a, tiles.at[q], tile_pass.at[a, q], tile_over, q).wait_send()
    for offset in order:
        p = member(me, offset, n)
        for a in range(2):
            col_copy(a, mine, p, p).wait_send()


def solution(mesh):
    n = mesh.shape["tile"]

    def on_device(coords, counts, segments):
        local_n, _, rows = coords.shape
        structs = local_n * mesh.shape["ens"]
        lanes = n * local_n
        blocks = rows // 8
        chunks = rows // CHUNK
        vmem, dma = pltpu.VMEM, pltpu.SemaphoreType.DMA
        out = pl.pallas_call(
            functools.partial(kernel, n, structs),
            out_shape=jax.ShapeDtypeStruct((3, local_n, rows), F32),
            in_specs=[
                pl.BlockSpec(memory_space=pltpu.VMEM),
                pl.BlockSpec(memory_space=pl.ANY),
                pl.BlockSpec(memory_space=pltpu.VMEM),
            ],
            out_specs=pl.BlockSpec(memory_space=pltpu.VMEM),
            scratch_shapes=[
                vmem((chunks, local_n, LANES), F32),
                vmem((n, chunks, local_n, LANES), F32),
                vmem((n, chunks, local_n, LANES), F32),
                vmem((n, chunks, local_n, LANES), F32),
                vmem((3 * rows, lanes), F32),
                vmem((3 * rows, lanes), F32),
                vmem((rows, lanes), F32),
                vmem((rows, lanes), F32),
                vmem((blocks, blocks, 8, 8, lanes), F32),
                vmem((rows, WINDOW), jnp.int32),
                vmem((chunks, rows, LANES), F32),
                vmem((chunks, rows, LANES), F32),
                vmem((chunks, rows, LANES), F32),
                vmem((chunks, rows, LANES), F32),
                vmem((chunks, rows, LANES), F32),
                vmem((LANES, lanes), F32),
                vmem((chunks, n, local_n, LANES), F32),
                vmem((chunks, n, local_n, LANES), F32),
                dma((2, n)), dma((2, n)), dma((2, n)), dma((n,)), dma((n,)), dma((n,)), dma((2, n)), dma((2, n)),
                dma((chunks,)), dma((chunks,)), dma((chunks, n)), dma((chunks, n)), dma,
            ],
            compiler_params=pltpu.CompilerParams(
                collective_id=0, has_side_effects=True, vmem_limit_bytes=60 * 1024 * 1024
            ),
        )(coords.transpose(1, 0, 2), counts, segments.reshape(1, -1))
        return out.transpose(1, 0, 2)

    return jax.shard_map(
        on_device,
        mesh=mesh,
        in_specs=(P("ens", None, "tile"), P("tile", None), P()),
        out_specs=P("ens", None, "tile"),
        check_vma=False,
    )
```
